32 devices in a mesh: member: 4 (over y, core), lon: 4 (over z), lat: 2 (over x).
Axes of the slice: x: 2, y: 2, z: 4, core: 2. Of those that a mesh axis runs over, the one named last changes fastest.
Arguments:
- member_state: float32 [4, 16, 256, 1536], P('member', None, 'lat', 'lon'), may hold values from -12 to 12
- column_depth: float32 [256, 1536], P('lat', 'lon'), may hold values from 0.5 to 2
- rotation: float32 [256, 1536], P('lat', 'lon'), may hold values from -0.2 to 0.2
- diffusivity: float32 [5, 256, 1536], P(None, 'lat', 'lon'), may hold values from 0.02 to 0.2
- ocean_mask: int32 [256, 1536], P('lat', 'lon'), may hold values from 0 to 1, as said below
- region_id: int32 [256, 1536], P('lat', 'lon'), may hold values from 0 to 15, as said below
- target_rms: float32 [16], replicated, may hold values from 0.2 to 1
Outputs:
- bred_state: float32 [4, 16, 256, 1536], P('member', None, 'lat', 'lon')
- growth_rms: float32 [4, 16], P('member')
The draws below stay inside these ranges and needn't reach their ends.
Inputs may be any that keep to these rules, and one draw needn't show every extreme that they name: `ocean_mask`: 1 marks an ocean cell. `region_id`: every region id holds ocean cells.
All inputs are finite; a program needn't handle non-finite values.
Results may differ from the reference program's by a relative error of at most 0.0003.
Values sent between devices are 32-bit elements; how exact they have to be, the bound alone decides.
A program may use at most 64 MiB of HBM per device.

```python
import math
import jax
import jax.numpy as jnp
from jax import lax

LEV = 5
STEPS = 2
SECTORS = 8
MEMBERS = 4
CHANNELS = 16
REGIONS = 16
NLAT = 256
NLON = 1536


def draw_member_state(key, part):
    keys = jax.random.split(key, 2)
    shape = (MEMBERS, CHANNELS, NLAT, NLON)
    ramp = jnp.exp(math.log(3.0) * jnp.arange(NLON).astype(jnp.float32) / NLON)[None, None, None, :]
    rows = jnp.exp(jax.random.uniform(keys[0], (1, 1, NLAT, 1), jnp.float32, 0.0, math.log(3.3)))
    scale = 0.3 * rows * ramp
    return jax.random.truncated_normal(keys[1], -4.0, 4.0, shape, jnp.float32) * scale


def draw_ocean_mask(key, part):
    coins = jax.random.randint(key, (NLAT, NLON), 0, 4)
    rows = jnp.arange(NLAT)[:, None]
    ocean = jnp.where(coins > 0, 1, 0)
    edge = (rows == 0) | (rows == NLAT - 1)
    return jnp.where(edge, 1, ocean).astype(jnp.int32)


def draw_region_id(key, part):
    keys = jax.random.split(key, 2)
    offset = jax.random.randint(keys[0], (NLAT, 1), 0, SECTORS)
    columns = jnp.arange(NLON)[None, :]
    block_width = max(NLON // (4 * SECTORS), 1)
    sector = (columns // block_width + offset) % SECTORS
    bound = jax.random.randint(keys[1], (1, NLON), NLAT // 4, 3 * NLAT // 4 + 1)
    rows = jnp.arange(NLAT)[:, None]
    return (sector * 2 + jnp.where(rows >= bound, 1, 0)).astype(jnp.int32)


def block_scale(own_key, dims, cuts, low, top_value):
    level, own = 1.0, jax.random.fold_in(own_key, 6)
    for dim, shards_of in cuts:
        steps = jnp.exp(jax.random.uniform(jax.random.fold_in(own, dim), (shards_of,), jnp.float32, low / len(cuts), top_value / len(cuts)))
        level = level * jnp.repeat(steps, dims[dim] // shards_of).reshape([-1 if axis == dim else 1 for axis in range(len(dims))])
    return level


def setup_inputs(seed: int = 0) -> dict:
    key_list = jax.random.split(jax.random.key(seed), 8)
    return {
        "member_state": draw_member_state(jax.random.fold_in(key_list[7], 71), 0),
        "column_depth": jnp.clip(jnp.exp(math.log(2.0) - 1.3862944 * jax.random.uniform(key_list[1], (NLAT, NLON), jnp.float32) ** block_scale(key_list[1], (NLAT, NLON), ((0, 2), (1, 4)), -0.2, 0.2)), 0.5, 2.0),
        "rotation": jnp.clip(jax.random.uniform(key_list[2], (NLAT, NLON), jnp.float32, -0.2, 0.2) * block_scale(key_list[2], (NLAT, NLON), ((0, 2), (1, 4)), -0.4, 0.0), -0.2, 0.2),
        "diffusivity": jnp.clip(jnp.exp(math.log(0.2) - 2.3025851 * jax.random.uniform(key_list[3], (LEV, NLAT, NLON), jnp.float32) ** block_scale(key_list[3], (LEV, NLAT, NLON), ((1, 2), (2, 4)), -0.2, 0.2)), 0.02, 0.2),
        "ocean_mask": draw_ocean_mask(jax.random.fold_in(key_list[7], 71), 0),
        "region_id": draw_region_id(jax.random.fold_in(key_list[7], 71), 0),
        "target_rms": jnp.clip(jnp.exp(jax.random.uniform(key_list[6], (REGIONS,), jnp.float32, math.log(0.2), math.log(1.0))), 0.2, 1.0),
    }


divergence_gain = 0.25
pressure_gain = 0.25
buoyancy_gain = 0.1
advection_gain = 0.05
epsilon = 1e-06

def neighbours(field):
    east_side = jnp.roll(field, -1, axis=-1)
    west_side = jnp.roll(field, 1, axis=-1)
    zero_row = jnp.zeros_like(field[..., :1, :])
    north_side = jnp.concatenate([field[..., 1:, :], zero_row], axis=-2)
    south_side = jnp.concatenate([zero_row, field[..., :-1, :]], axis=-2)
    return (east_side, west_side, north_side, south_side)

def advance(state, column_depth, rotation, diffusivity, ocean_float):
    east_side, west_side, north_side, south_side = neighbours(state)
    zonal_diff = east_side - west_side
    merid_diff = north_side - south_side
    laplacian = east_side + west_side + north_side + south_side - 4.0 * state
    surface = state[:, 0]
    zonal_flow = state[:, 1:1 + LEV]
    merid_flow = state[:, 1 + LEV:1 + 2 * LEV]
    heat_field = state[:, 1 + 2 * LEV:]
    divergence = lax.optimization_barrier(jnp.mean(zonal_diff[:, 1:1 + LEV], axis=1)) + lax.optimization_barrier(jnp.mean(merid_diff[:, 1 + LEV:1 + 2 * LEV], axis=1))
    new_surface = ocean_float * (surface - divergence_gain * column_depth * divergence)
    s_east, s_west, s_north, s_south = neighbours(new_surface)
    slope_east = (s_east - s_west)[:, None]
    slope_north = (s_north - s_south)[:, None]
    heat_east = zonal_diff[:, 1 + 2 * LEV:]
    heat_north = merid_diff[:, 1 + 2 * LEV:]
    new_zonal = ocean_float * (zonal_flow + rotation * merid_flow - pressure_gain * slope_east - buoyancy_gain * heat_east + diffusivity * laplacian[:, 1:1 + LEV])
    new_merid = ocean_float * (merid_flow - rotation * zonal_flow - pressure_gain * slope_north - buoyancy_gain * heat_north + diffusivity * laplacian[:, 1 + LEV:1 + 2 * LEV])
    new_heat = ocean_float * (heat_field + diffusivity * laplacian[:, 1 + 2 * LEV:] - advection_gain * (new_zonal * heat_east + new_merid * heat_north))
    return jnp.concatenate([new_surface[:, None], new_zonal, new_merid, new_heat], axis=1)

def reference(member_state, column_depth, rotation, diffusivity, ocean_mask, region_id, target_rms):
    ocean_float = ocean_mask.astype(jnp.float32)
    state = member_state
    for step_index in range(STEPS):
        state = advance(state, column_depth, rotation, diffusivity, ocean_float)
    control = state[0:1]
    difference = state - control
    cell_sum = ocean_float * lax.optimization_barrier(jnp.sum(difference * difference, axis=1))
    labels = jnp.arange(REGIONS).astype(jnp.int32)
    onehot = (region_id[None] == labels[:, None, None]).astype(jnp.float32)
    squares = jnp.einsum('rji,mji->mr', onehot, cell_sum, precision=lax.Precision.HIGHEST)
    counts = jnp.einsum('rji,ji->r', onehot, ocean_float, precision=lax.Precision.HIGHEST)
    growth = jnp.sqrt(squares / (counts * CHANNELS) + epsilon)
    factor = target_rms[None] / growth
    cell_factor = jnp.einsum('mr,rji->mji', factor, onehot, precision=lax.Precision.HIGHEST)
    bred = control + cell_factor[:, None] * difference
    return (bred, growth)
```

```python
import functools

import jax
import jax.numpy as jnp
from jax import lax
from jax.experimental import pallas as pl
from jax.experimental.pallas import tpu as pltpu
from jax.sharding import PartitionSpec as P

LEV = 5
STEPS = 2
MARGIN = 2 * STEPS
TILE = 8
LANES = 128

divergence_gain = 0.25
pressure_gain = 0.25
buoyancy_gain = 0.1
advection_gain = 0.05
epsilon = 1e-06

MESH = pl.DeviceIdType.MESH


def chunk_tiles(rows):
    tiles = rows // TILE
    return 2 if tiles % 2 == 0 else 1


def cycle_kernel(
    sizes,
    state_in, depth_in, rotation_in, diffusivity_in, mask_in, region_in,
    own_out, control_out, growth_out,
    field, middle, own, control, mask, region, surface, merid_sum,
    send_east, send_west, from_east, from_west,
    send_north, send_south, from_north, from_south,
    squares, counts, gathered,
    in_sem, halo_send, halo_recv, cast_send, cast_recv, out_sem, sum_send, sum_recv,
):
    members, lons, lats = sizes
    channels, rows, columns = state_in.shape
    regions = growth_out.shape[0]
    fields = field.shape[0]
    wide = columns + LANES
    tiles = rows // TILE
    per_chunk = chunk_tiles(rows)
    chunk_rows = per_chunk * TILE
    chunks = rows // chunk_rows
    DEPTH, ROT, OCEAN, DIFF = channels, channels + 1, channels + 2, channels + 3

    me = lax.axis_index("member")
    lon = lax.axis_index("lon")
    lat = lax.axis_index("lat")

    def at(dlat, dlon):
        return {
            "member": me,
            "lon": lax.rem(lon + dlon + lons, lons),
            "lat": lax.rem(lat + dlat + lats, lats),
        }

    def to_member(other):
        return {"member": other, "lon": lon, "lat": lat}

    inner = (slice(TILE, TILE + rows), slice(0, columns))
    loads = [
        pltpu.make_async_copy(state_in, field.at[(slice(0, channels),) + inner], in_sem.at[0]),
        pltpu.make_async_copy(depth_in, field.at[(DEPTH,) + inner], in_sem.at[1]),
        pltpu.make_async_copy(rotation_in, field.at[(ROT,) + inner], in_sem.at[2]),
        pltpu.make_async_copy(diffusivity_in, field.at[(slice(DIFF, fields),) + inner], in_sem.at[3]),
        pltpu.make_async_copy(mask_in, mask, in_sem.at[4]),
        pltpu.make_async_copy(region_in, region, in_sem.at[5]),
    ]
    for load in loads:
        load.start()

    peers = [(a, b) for a in range(lats) for b in range(lons) if (a, b) != (0, 0)]
    barrier = pltpu.get_barrier_semaphore()
    for a, b in peers:
        pl.semaphore_signal(barrier, inc=1, device_id=at(a, b), device_id_type=MESH)
    even = lax.rem(me, 2) == 0
    has_pair = even & (me + 1 < members)
    has_next = even & (me + 2 < members)
    parent = jnp.where(even, me - 2, me - 1)

    @pl.when(me > 0)
    def _():
        pl.semaphore_signal(barrier, inc=1, device_id=to_member(parent), device_id_type=MESH)

    pl.semaphore_wait(
        barrier, len(peers) + has_pair.astype(jnp.int32) + has_next.astype(jnp.int32)
    )

    for load in loads:
        load.wait()

    lane = lax.broadcasted_iota(jnp.int32, (TILE, LANES), 1)
    sub = lax.broadcasted_iota(jnp.int32, (TILE, columns), 0)
    zero_tile = jnp.zeros((TILE, LANES), jnp.float32)

    def make_ocean(t, carry):
        r = pl.multiple_of(t * TILE, TILE)
        field[OCEAN, pl.ds(r + TILE, TILE), 0:columns] = mask[pl.ds(r, TILE), :].astype(jnp.float32)
        return carry

    lax.fori_loop(0, tiles, make_ocean, 0)

    for k in range(fields // 2):
        a, b = 2 * k, 2 * k + 1
        top = slice(rows, rows + TILE)
        low = slice(TILE, 2 * TILE)
        half = TILE // 2
        send_north[k] = jnp.where(
            sub < half, pltpu.roll(field[a, top, 0:columns], half, 0), field[b, top, 0:columns]
        )
        send_south[k] = jnp.where(
            sub < half, field[a, low, 0:columns], pltpu.roll(field[b, low, 0:columns], half, 0)
        )

    def remote(src, dst, index, device):
        return pltpu.make_async_remote_copy(
            src_ref=src, dst_ref=dst, send_sem=halo_send.at[index], recv_sem=halo_recv.at[index],
            device_id=device, device_id_type=MESH,
        )

    has_north = lat < lats - 1
    has_south = lat > 0
    whole = slice(TILE, TILE + rows)
    last = slice(rows - TILE, rows)
    first = slice(0, TILE)
    above = slice(rows + TILE, rows + 2 * TILE)
    north = [remote(send_north, from_south, 0, at(1, 0))]
    south = [remote(send_south, from_north, 1, at(-1, 0))]
    sideways = [
        remote(send_east, from_west.at[whole], 2, at(0, 1)),
        remote(send_west, from_east.at[whole], 3, at(0, -1)),
    ]
    north_corners = [
        remote(send_east.at[last], from_west.at[first], 4, at(1, 1)),
        remote(send_west.at[last], from_east.at[first], 5, at(1, -1)),
    ]
    south_corners = [
        remote(send_east.at[first], from_west.at[above], 6, at(-1, 1)),
        remote(send_west.at[first], from_east.at[above], 7, at(-1, -1)),
    ]

    @pl.when(has_north)
    def _():
        for copy in north:
            copy.start()

    @pl.when(has_south)
    def _():
        for copy in south:
            copy.start()

    def pack(t, carry):
        r = pl.multiple_of(t * TILE, TILE)
        east, west = zero_tile, zero_tile
        for f in range(fields):
            here = (lane >= MARGIN * f) & (lane < MARGIN * (f + 1))
            edge = field[f, pl.ds(r + TILE, TILE), columns - LANES : columns]
            east = jnp.where(here, pltpu.roll(edge, (MARGIN * f + MARGIN) % LANES, 1), east)
            edge = field[f, pl.ds(r + TILE, TILE), 0:LANES]
            west = jnp.where(here, pltpu.roll(edge, MARGIN * f, 1) if f else edge, west)
        send_east[pl.ds(r, TILE), :] = east
        send_west[pl.ds(r, TILE), :] = west
        return carry

    lax.fori_loop(0, tiles, pack, 0)
    for copy in sideways:
        copy.start()

    @pl.when(has_north)
    def _():
        for copy in north_corners:
            copy.start()

    @pl.when(has_south)
    def _():
        for copy in south_corners:
            copy.start()

    def clear(ref):
        for k in range(regions):
            ref[k] = zero_tile

    def add_regions(ref, r, value):
        ids = region[pl.ds(r, TILE), :]
        for k in range(regions):
            picked = jnp.where(ids == k, value, 0.0)
            total = picked[:, 0:LANES]
            for c in range(LANES, columns, LANES):
                total = total + picked[:, c : c + LANES]
            ref[k] = ref[k] + total

    def share(ref, which):
        gathered[which, 0] = jnp.sum(ref[...], axis=1)
        for p, (a, b) in enumerate(peers):
            pltpu.make_async_remote_copy(
                src_ref=gathered.at[which, 0], dst_ref=gathered.at[which, p + 1],
                send_sem=sum_send.at[which, p], recv_sem=sum_recv.at[which, p],
                device_id=at(a, b), device_id_type=MESH,
            ).start()

    def collect(which):
        for p, (a, b) in enumerate(peers):
            pltpu.make_async_remote_copy(
                src_ref=gathered.at[which, 0], dst_ref=gathered.at[which, p + 1],
                send_sem=sum_send.at[which, p], recv_sem=sum_recv.at[which, p],
                device_id=at(a, b), device_id_type=MESH,
            ).wait()
        total = gathered[which, 0]
        for p in range(len(peers)):
            total = total + gathered[which, p + 1]
        return jnp.sum(total, axis=1, keepdims=True)

    clear(squares)
    clear(counts)

    def count(t, carry):
        r = pl.multiple_of(t * TILE, TILE)
        add_regions(counts, r, field[OCEAN, pl.ds(r + TILE, TILE), 0:columns])
        return carry

    lax.fori_loop(0, tiles, count, 0)
    share(counts, 0)

    for copy in sideways:
        copy.wait()

    @pl.when(has_north)
    def _():
        for copy in north + north_corners:
            copy.wait_send()
        for copy in south + south_corners:
            copy.wait_recv()

    @pl.when(has_south)
    def _():
        for copy in south + south_corners:
            copy.wait_send()
        for copy in north + north_corners:
            copy.wait_recv()

    @pl.when(jnp.logical_not(has_north))
    def _():
        from_north[...] = jnp.zeros_like(from_north)
        from_east[above, :] = zero_tile
        from_west[above, :] = zero_tile

    @pl.when(jnp.logical_not(has_south))
    def _():
        from_south[...] = jnp.zeros_like(from_south)
        from_east[first, :] = zero_tile
        from_west[first, :] = zero_tile

    for k in range(fields // 2):
        a, b = 2 * k, 2 * k + 1
        field[a, first, 0:columns] = pltpu.roll(from_south[k], TILE // 2, 0)
        field[b, first, 0:columns] = from_south[k]
        field[a, above, 0:columns] = from_north[k]
        field[b, above, 0:columns] = pltpu.roll(from_north[k], TILE // 2, 0)

    def unpack(t, carry):
        r = pl.multiple_of(t * TILE, TILE)
        east = from_east[pl.ds(r, TILE), :]
        west = from_west[pl.ds(r, TILE), :]
        for f in range(fields):
            to_first = pltpu.roll(east, LANES - MARGIN * f, 1) if f else east
            to_last = pltpu.roll(west, LANES - MARGIN - MARGIN * f, 1)
            field[f, pl.ds(r, TILE), columns:wide] = jnp.where(lane < MARGIN, to_first, to_last)
        return carry

    lax.fori_loop(0, tiles + 2, unpack, 0)

    sub_wide = lax.broadcasted_iota(jnp.int32, (TILE, wide), 0)

    def starts(t):
        r = pl.multiple_of(t * TILE, TILE)
        before = pl.multiple_of(jnp.maximum(t - 1, 0) * TILE, TILE)
        after = pl.multiple_of(jnp.minimum(t + 1, tiles + 1) * TILE, TILE)
        return r, before, after

    def east_west(q, width):
        return (
            pltpu.roll(q, wide - 1, 1)[:, 0:width],
            pltpu.roll(q, 1, 1)[:, 0:width],
        )

    def north_south(q, below, beyond):
        rows_of = sub_wide[:, 0 : q.shape[1]]
        return (
            pltpu.roll(jnp.where(rows_of == 0, beyond, q), TILE - 1, 0),
            pltpu.roll(jnp.where(rows_of == TILE - 1, below, q), 1, 0),
        )

    def add_up(ref, base, r):
        total = ref[base, pl.ds(r, TILE), :]
        for k in range(1, LEV):
            total = total + ref[base + k, pl.ds(r, TILE), :]
        return total

    def merid_pass(src):
        def body(t, carry):
            r = pl.multiple_of(t * TILE, TILE)
            merid_sum[pl.ds(r, TILE), :] = add_up(src, 1 + LEV, r)
            return carry

        lax.fori_loop(0, tiles + 2, body, 0)

    def surface_pass(src):
        def body(t, carry):
            r, before, after = starts(t)
            e, w = east_west(add_up(src, 1, r), wide)
            n, s = north_south(
                merid_sum[pl.ds(r, TILE), :],
                merid_sum[pl.ds(before, TILE), :],
                merid_sum[pl.ds(after, TILE), :],
            )
            divergence = (e - w) + (n - s)
            now = pl.ds(r, TILE)
            surface[now, :] = field[OCEAN, now, :] * (
                src[0, now, :] - (divergence_gain / LEV) * field[DEPTH, now, :] * divergence
            )
            return carry

        lax.fori_loop(0, tiles + 2, body, 0)

    def update_tile(src, t, width, write):
        r, before, after = starts(t)
        now, below, beyond = pl.ds(r, TILE), pl.ds(before, TILE), pl.ds(after, TILE)

        def around(ref, *index):
            whole_q = ref[(*index, now, slice(None))]
            q = whole_q[:, 0:width]
            e, w = east_west(whole_q, width)
            n, s = north_south(
                q, ref[(*index, below, slice(0, width))], ref[(*index, beyond, slice(0, width))]
            )
            return q, e, w, n, s

        new_surface, e, w, n, s = around(surface)
        slope_east = pressure_gain * (e - w)
        slope_north = pressure_gain * (n - s)
        ocean = field[OCEAN, now, 0:width]
        rotation = field[ROT, now, 0:width]
        write(0, r, new_surface)
        for k in range(LEV):
            mixing = field[DIFF + k, now, 0:width]
            u, ue, uw, un, us = around(src, 1 + k)
            v, ve, vw, vn, vs = around(src, 1 + LEV + k)
            c, ce, cw, cn, cs = around(src, 1 + 2 * LEV + k)
            heat_east = ce - cw
            heat_north = cn - cs
            new_u = ocean * (
                u + rotation * v - slope_east - buoyancy_gain * heat_east
                + mixing * (((ue + uw) + (un + us)) - 4.0 * u)
            )
            new_v = ocean * (
                v - rotation * u - slope_north - buoyancy_gain * heat_north
                + mixing * (((ve + vw) + (vn + vs)) - 4.0 * v)
            )
            new_c = ocean * (
                c + mixing * (((ce + cw) + (cn + cs)) - 4.0 * c)
                - advection_gain * (new_u * heat_east + new_v * heat_north)
            )
            write(1 + k, r, new_u)
            write(1 + LEV + k, r, new_v)
            write(1 + 2 * LEV + k, r, new_c)

    merid_pass(field)
    surface_pass(field)

    def first_step(t, carry):
        def write(channel, r, value):
            middle[channel, pl.ds(r, TILE), :] = value

        update_tile(field, t, wide, write)
        return carry

    lax.fori_loop(0, tiles + 2, first_step, 0)
    merid_pass(middle)
    surface_pass(middle)

    def cast(c, which, device):
        part = control.at[:, pl.ds(pl.multiple_of(c * chunk_rows, TILE), chunk_rows), :]
        return pltpu.make_async_remote_copy(
            src_ref=part, dst_ref=part, send_sem=cast_send.at[which, c], recv_sem=cast_recv.at[c],
            device_id=to_member(device), device_id_type=MESH,
        )

    def pass_on(c):
        @pl.when(has_next)
        def _():
            cast(c, 1, me + 2).start()

        @pl.when(has_pair)
        def _():
            cast(c, 0, me + 1).start()

    def save(c, which):
        part = pl.ds(pl.multiple_of(c * chunk_rows, TILE), chunk_rows)
        src, dst = (own, own_out) if which == 0 else (control, control_out)
        return pltpu.make_async_copy(src.at[:, part, :], dst.at[:, part, :], out_sem.at[which, c])

    def second_step(c, carry):
        def one(j, inner_carry):
            def write(channel, r, value):
                own[channel, pl.ds(r - TILE, TILE), :] = value

            update_tile(middle, c * per_chunk + j + 1, columns, write)
            return inner_carry

        lax.fori_loop(0, per_chunk, one, 0)
        save(c, 0).start()

        @pl.when(me == 0)
        def _():
            part = pl.ds(pl.multiple_of(c * chunk_rows, TILE), chunk_rows)
            for k in range(channels):
                control[k, part, :] = own[k, part, :]
            pass_on(c)

        return carry

    lax.fori_loop(0, chunks, second_step, 0)

    def compare(c, carry):
        @pl.when(me > 0)
        def _():
            cast(c, 0, me).wait_recv()
            pass_on(c)

        save(c, 1).start()

        def one(j, inner_carry):
            r = pl.multiple_of(c * chunk_rows + j * TILE, TILE)
            total = None
            for k in range(channels):
                d = own[k, pl.ds(r, TILE), :] - control[k, pl.ds(r, TILE), :]
                total = d * d if total is None else total + d * d
            add_regions(squares, r, field[OCEAN, pl.ds(r + TILE, TILE), 0:columns] * total)
            return inner_carry

        lax.fori_loop(0, per_chunk, one, 0)
        return carry

    lax.fori_loop(0, chunks, compare, 0)
    share(squares, 1)
    count_sum = collect(0)

    def finish(c, carry):
        save(c, 0).wait()
        save(c, 1).wait()

        @pl.when(has_next)
        def _():
            cast(c, 1, me + 2).wait_send()

        @pl.when(has_pair)
        def _():
            cast(c, 0, me + 1).wait_send()

        return carry

    lax.fori_loop(0, chunks, finish, 0)
    square_sum = collect(1)
    growth = jnp.sqrt(square_sum / (count_sum * channels) + epsilon)
    growth_out[...] = jnp.broadcast_to(growth, growth_out.shape)


def breed_kernel(target, region, own, control, growth_in, bred, growth):
    regions = growth_in.shape[0]
    channels, rows, columns = own.shape
    ids = region[...]
    factor = jnp.zeros(ids.shape, jnp.float32)
    for k in range(regions):
        value = target[k] / growth_in[k : k + 1, :]
        value = jnp.concatenate([value] * (columns // LANES), axis=1)
        factor = jnp.where(ids == k, jnp.broadcast_to(value, ids.shape), factor)
    for k in range(channels):
        base = control[k]
        bred[k] = base + factor * (own[k] - base)
    shape = growth_in.shape
    diagonal = lax.broadcasted_iota(jnp.int32, shape, 0) == lax.broadcasted_iota(jnp.int32, shape, 1)
    line = jnp.sum(jnp.where(diagonal, growth_in[...], 0.0), axis=0, keepdims=True)
    growth[...] = line[:, 0 : growth.shape[1]]


def per_device(
    sizes, member_state, column_depth, rotation, diffusivity, ocean_mask, region_id, target_rms
):
    members, lons, lats = sizes
    _, channels, rows, columns = member_state.shape
    regions = target_rms.shape[0]
    fields = channels + 3 + LEV
    tall, wide = rows + 2 * TILE, columns + LANES
    chunks = rows // (chunk_tiles(rows) * TILE)
    group = lons * lats
    f32 = jnp.float32
    anywhere = pl.BlockSpec(memory_space=pl.ANY)
    own, control, growth_wide = pl.pallas_call(
        functools.partial(cycle_kernel, sizes),
        out_shape=(
            jax.ShapeDtypeStruct((channels, rows, columns), f32),
            jax.ShapeDtypeStruct((channels, rows, columns), f32),
            jax.ShapeDtypeStruct((regions, LANES), f32),
        ),
        in_specs=[anywhere] * 6,
        out_specs=(anywhere, anywhere, pl.BlockSpec(memory_space=pltpu.VMEM)),
        scratch_shapes=[
            pltpu.VMEM((fields, tall, wide), f32),
            pltpu.VMEM((channels, tall, wide), f32),
            pltpu.VMEM((channels, rows, columns), f32),
            pltpu.VMEM((channels, rows, columns), f32),
            pltpu.VMEM((rows, columns), jnp.int32),
            pltpu.VMEM((rows, columns), jnp.int32),
            pltpu.VMEM((tall, wide), f32),
            pltpu.VMEM((tall, wide), f32),
            pltpu.VMEM((rows, LANES), f32),
            pltpu.VMEM((rows, LANES), f32),
            pltpu.VMEM((tall, LANES), f32),
            pltpu.VMEM((tall, LANES), f32),
            pltpu.VMEM((fields // 2, TILE, columns), f32),
            pltpu.VMEM((fields // 2, TILE, columns), f32),
            pltpu.VMEM((fields // 2, TILE, columns), f32),
            pltpu.VMEM((fields // 2, TILE, columns), f32),
            pltpu.VMEM((regions, TILE, LANES), f32),
            pltpu.VMEM((regions, TILE, LANES), f32),
            pltpu.VMEM((2, group, regions, LANES), f32),
            pltpu.SemaphoreType.DMA((6,)),
            pltpu.SemaphoreType.DMA((8,)),
            pltpu.SemaphoreType.DMA((8,)),
            pltpu.SemaphoreType.DMA((2, chunks)),
            pltpu.SemaphoreType.DMA((chunks,)),
            pltpu.SemaphoreType.DMA((2, chunks)),
            pltpu.SemaphoreType.DMA((2, group - 1)),
            pltpu.SemaphoreType.DMA((2, group - 1)),
        ],
        compiler_params=pltpu.CompilerParams(collective_id=0, has_side_effects=True),
    )(
        member_state.reshape(channels, rows, columns),
        column_depth, rotation, diffusivity, ocean_mask, region_id,
    )
    block = 32 if rows % 32 == 0 else rows
    volume = pl.BlockSpec((channels, block, columns), lambda i: (0, i, 0))
    bred, growth = pl.pallas_call(
        breed_kernel,
        grid=(rows // block,),
        out_shape=(
            jax.ShapeDtypeStruct((channels, rows, columns), f32),
            jax.ShapeDtypeStruct((1, regions), f32),
        ),
        in_specs=[
            pl.BlockSpec(memory_space=pltpu.SMEM),
            pl.BlockSpec((block, columns), lambda i: (i, 0)),
            volume,
            volume,
            pl.BlockSpec((regions, LANES), lambda i: (0, 0)),
        ],
        out_specs=(volume, pl.BlockSpec((1, regions), lambda i: (0, 0))),
    )(target_rms, region_id, own, control, growth_wide)
    return (bred[None], growth)


def solution(mesh):
    sizes = (mesh.shape["member"], mesh.shape["lon"], mesh.shape["lat"])
    return jax.shard_map(
        functools.partial(per_device, sizes),
        mesh=mesh,
        in_specs=(
            P("member", None, "lat", "lon"),
            P("lat", "lon"),
            P("lat", "lon"),
            P(None, "lat", "lon"),
            P("lat", "lon"),
            P("lat", "lon"),
            P(),
        ),
        out_specs=(P("member", None, "lat", "lon"), P("member", None)),
        check_vma=False,
    )
```

```python
import functools

import jax
import jax.numpy as jnp
from jax import lax
from jax.experimental import pallas as pl
from jax.experimental.pallas import tpu as pltpu
from jax.sharding import PartitionSpec as P

LEV = 5
STEPS = 2
MARGIN = 2 * STEPS
TILE = 8
LANES = 128
EARLY = 6

divergence_gain = 0.25
pressure_gain = 0.25
buoyancy_gain = 0.1
advection_gain = 0.05
epsilon = 1e-06

MESH = pl.DeviceIdType.MESH


def cycle_kernel(
    sizes,
    state_in, depth_in, rotation_in, diffusivity_in, mask_in, region_in,
    own_out, control_out, growth_out,
    field, middle, raw, own, control, mask, region,
    surface_one, surface_two, merid_one, merid_two,
    send_east, send_west, from_east, from_west,
    send_north, send_south, from_north, from_south,
    raw_east, raw_west, raw_north, raw_south,
    squares, counts, gathered,
    in_sem, halo_send, halo_recv, raw_send, raw_recv, rim_send, rim_recv,
    cast_send, cast_recv, out_sem, sum_send, sum_recv,
):
    members, lons, lats = sizes
    channels, rows, columns = state_in.shape
    regions = growth_out.shape[0]
    fields = field.shape[0]
    wide = columns + LANES
    tiles = rows // TILE
    tall_tiles = tiles + 2
    DEPTH, ROT, OCEAN, DIFF = channels, channels + 1, channels + 2, channels + 3

    me = lax.axis_index("member")
    lon = lax.axis_index("lon")
    lat = lax.axis_index("lat")

    def at(dlat, dlon):
        return {
            "member": me,
            "lon": lax.rem(lon + dlon + lons, lons),
            "lat": lax.rem(lat + dlat + lats, lats),
        }

    def to_member(other):
        return {"member": other, "lon": lon, "lat": lat}

    inner = (slice(TILE, TILE + rows), slice(0, columns))
    loads = [
        pltpu.make_async_copy(state_in, field.at[(slice(0, channels),) + inner], in_sem.at[0]),
        pltpu.make_async_copy(depth_in, field.at[(DEPTH,) + inner], in_sem.at[1]),
        pltpu.make_async_copy(rotation_in, field.at[(ROT,) + inner], in_sem.at[2]),
        pltpu.make_async_copy(diffusivity_in, field.at[(slice(DIFF, fields),) + inner], in_sem.at[3]),
        pltpu.make_async_copy(mask_in, mask, in_sem.at[4]),
        pltpu.make_async_copy(region_in, region, in_sem.at[5]),
    ]
    for load in loads:
        load.start()

    peers = [(a, b) for a in range(lats) for b in range(lons) if (a, b) != (0, 0)]
    barrier = pltpu.get_barrier_semaphore()
    for a, b in peers:
        pl.semaphore_signal(barrier, inc=1, device_id=at(a, b), device_id_type=MESH)
    even = lax.rem(me, 2) == 0
    has_pair = even & (me + 1 < members)
    has_next = even & (me + 2 < members)
    parent = jnp.where(even, me - 2, me - 1)

    @pl.when(me > 0)
    def _():
        pl.semaphore_signal(barrier, inc=1, device_id=to_member(parent), device_id_type=MESH)

    pl.semaphore_wait(
        barrier, len(peers) + has_pair.astype(jnp.int32) + has_next.astype(jnp.int32)
    )

    for load in loads:
        load.wait()

    early = min(EARLY, tiles)

    def cells(ref, t):
        return ref.at[0:channels, pl.ds(pl.multiple_of((t + 1) * TILE, TILE), TILE), 0:columns]

    def hand_down(src, t):
        return pltpu.make_async_remote_copy(
            src_ref=cells(src, t), dst_ref=cells(raw, t),
            send_sem=raw_send.at[t], recv_sem=raw_recv.at[t],
            device_id=to_member(me + 2), device_id_type=MESH,
        )

    def hand_down_some(begin, end):
        @pl.when((me == 0) & has_next)
        def _():
            def body(t, carry):
                hand_down(field, t).start()
                return carry

            lax.fori_loop(begin, end, body, 0)

    hand_down_some(0, early)

    lane = lax.broadcasted_iota(jnp.int32, (TILE, LANES), 1)
    sub = lax.broadcasted_iota(jnp.int32, (TILE, columns), 0)
    zero_tile = jnp.zeros((TILE, LANES), jnp.float32)

    def make_ocean(t, carry):
        r = pl.multiple_of(t * TILE, TILE)
        field[OCEAN, pl.ds(r + TILE, TILE), 0:columns] = mask[pl.ds(r, TILE), :].astype(jnp.float32)
        return carry

    lax.fori_loop(0, tiles, make_ocean, 0)

    for k in range(fields // 2):
        a, b = 2 * k, 2 * k + 1
        top = slice(rows, rows + TILE)
        low = slice(TILE, 2 * TILE)
        half = TILE // 2
        send_north[k] = jnp.where(
            sub < half, pltpu.roll(field[a, top, 0:columns], half, 0), field[b, top, 0:columns]
        )
        send_south[k] = jnp.where(
            sub < half, field[a, low, 0:columns], pltpu.roll(field[b, low, 0:columns], half, 0)
        )

    def remote(src, dst, index, device):
        return pltpu.make_async_remote_copy(
            src_ref=src, dst_ref=dst, send_sem=halo_send.at[index], recv_sem=halo_recv.at[index],
            device_id=device, device_id_type=MESH,
        )

    has_north = lat < lats - 1
    has_south = lat > 0
    whole = slice(TILE, TILE + rows)
    last = slice(rows - TILE, rows)
    first = slice(0, TILE)
    above = slice(rows + TILE, rows + 2 * TILE)
    north = [remote(send_north, from_south, 0, at(1, 0))]
    south = [remote(send_south, from_north, 1, at(-1, 0))]
    sideways = [
        remote(send_east, from_west.at[whole], 2, at(0, 1)),
        remote(send_west, from_east.at[whole], 3, at(0, -1)),
    ]
    north_corners = [
        remote(send_east.at[last], from_west.at[first], 4, at(1, 1)),
        remote(send_west.at[last], from_east.at[first], 5, at(1, -1)),
    ]
    south_corners = [
        remote(send_east.at[first], from_west.at[above], 6, at(-1, 1)),
        remote(send_west.at[first], from_east.at[above], 7, at(-1, -1)),
    ]

    @pl.when(has_north)
    def _():
        for copy in north:
            copy.start()

    @pl.when(has_south)
    def _():
        for copy in south:
            copy.start()

    def pack(t, carry):
        r = pl.multiple_of(t * TILE, TILE)
        east, west = zero_tile, zero_tile
        for f in range(fields):
            here = (lane >= MARGIN * f) & (lane < MARGIN * (f + 1))
            edge = field[f, pl.ds(r + TILE, TILE), columns - LANES : columns]
            east = jnp.where(here, pltpu.roll(edge, (MARGIN * f + MARGIN) % LANES, 1), east)
            edge = field[f, pl.ds(r + TILE, TILE), 0:LANES]
            west = jnp.where(here, pltpu.roll(edge, MARGIN * f, 1) if f else edge, west)
        send_east[pl.ds(r, TILE), :] = east
        send_west[pl.ds(r, TILE), :] = west
        return carry

    lax.fori_loop(0, tiles, pack, 0)
    for copy in sideways:
        copy.start()

    @pl.when(has_north)
    def _():
        for copy in north_corners:
            copy.start()

    @pl.when(has_south)
    def _():
        for copy in south_corners:
            copy.start()

    def clear(ref):
        for k in range(regions):
            ref[k] = zero_tile

    def add_regions(ref, r, value):
        ids = region[pl.ds(r, TILE), :]
        for k in range(regions):
            picked = jnp.where(ids == k, value, 0.0)
            total = picked[:, 0:LANES]
            for c in range(LANES, columns, LANES):
                total = total + picked[:, c : c + LANES]
            ref[k] = ref[k] + total

    def share(ref, which):
        gathered[which, 0] = jnp.sum(ref[...], axis=1)
        for p, (a, b) in enumerate(peers):
            pltpu.make_async_remote_copy(
                src_ref=gathered.at[which, 0], dst_ref=gathered.at[which, p + 1],
                send_sem=sum_send.at[which, p], recv_sem=sum_recv.at[which, p],
                device_id=at(a, b), device_id_type=MESH,
            ).start()

    def collect(which):
        for p, (a, b) in enumerate(peers):
            pltpu.make_async_remote_copy(
                src_ref=gathered.at[which, 0], dst_ref=gathered.at[which, p + 1],
                send_sem=sum_send.at[which, p], recv_sem=sum_recv.at[which, p],
                device_id=at(a, b), device_id_type=MESH,
            ).wait()
        total = gathered[which, 0]
        for p in range(len(peers)):
            total = total + gathered[which, p + 1]
        return jnp.sum(total, axis=1, keepdims=True)

    clear(squares)
    clear(counts)

    def count(t, carry):
        r = pl.multiple_of(t * TILE, TILE)
        add_regions(counts, r, field[OCEAN, pl.ds(r + TILE, TILE), 0:columns])
        return carry

    lax.fori_loop(0, tiles, count, 0)
    share(counts, 0)

    for copy in sideways:
        copy.wait()

    @pl.when(has_north)
    def _():
        for copy in north + north_corners:
            copy.wait_send()
        for copy in south + south_corners:
            copy.wait_recv()

    @pl.when(has_south)
    def _():
        for copy in south + south_corners:
            copy.wait_send()
        for copy in north + north_corners:
            copy.wait_recv()

    @pl.when(jnp.logical_not(has_north))
    def _():
        from_north[...] = jnp.zeros_like(from_north)
        from_east[above, :] = zero_tile
        from_west[above, :] = zero_tile

    @pl.when(jnp.logical_not(has_south))
    def _():
        from_south[...] = jnp.zeros_like(from_south)
        from_east[first, :] = zero_tile
        from_west[first, :] = zero_tile

    pairs = channels // 2

    def rims(east, west, above_rows, below_rows):
        def rim(src, dst, index):
            return pltpu.make_async_remote_copy(
                src_ref=src, dst_ref=dst, send_sem=rim_send.at[index], recv_sem=rim_recv.at[index],
                device_id=to_member(me + 2), device_id_type=MESH,
            )

        return (
            rim(east, raw_east, 0),
            rim(west, raw_west, 1),
            rim(above_rows, raw_north, 2),
            rim(below_rows, raw_south, 3),
        )

    own_rims = rims(from_east, from_west, from_north.at[0:pairs], from_south.at[0:pairs])
    raw_rims = rims(raw_east, raw_west, raw_north, raw_south)

    def start_rims(copies):
        copies[0].start()
        copies[1].start()

        @pl.when(has_north)
        def _():
            copies[2].start()

        @pl.when(has_south)
        def _():
            copies[3].start()

    @pl.when((me == 0) & has_next)
    def _():
        start_rims(own_rims)

    hand_down_some(early, tiles)

    def edge_rows(ref, above_rows, below_rows, count):
        for k in range(count):
            a, b = 2 * k, 2 * k + 1
            ref[a, first, 0:columns] = pltpu.roll(below_rows[k], TILE // 2, 0)
            ref[b, first, 0:columns] = below_rows[k]
            ref[a, above, 0:columns] = above_rows[k]
            ref[b, above, 0:columns] = pltpu.roll(above_rows[k], TILE // 2, 0)

    def edge_columns(ref, east_ref, west_ref, count, t):
        r = pl.multiple_of(t * TILE, TILE)
        east = east_ref[pl.ds(r, TILE), :]
        west = west_ref[pl.ds(r, TILE), :]
        for f in range(count):
            to_first = pltpu.roll(east, LANES - MARGIN * f, 1) if f else east
            to_last = pltpu.roll(west, LANES - MARGIN - MARGIN * f, 1)
            ref[f, pl.ds(r, TILE), columns:wide] = jnp.where(lane < MARGIN, to_first, to_last)

    sub_wide = lax.broadcasted_iota(jnp.int32, (TILE, wide), 0)

    def starts(t):
        r = pl.multiple_of(t * TILE, TILE)
        before = pl.multiple_of(jnp.maximum(t - 1, 0) * TILE, TILE)
        after = pl.multiple_of(jnp.minimum(t + 1, tiles + 1) * TILE, TILE)
        return r, before, after

    def east_west(q, width):
        return (
            pltpu.roll(q, wide - 1, 1)[:, 0:width],
            pltpu.roll(q, 1, 1)[:, 0:width],
        )

    def north_south(q, below, beyond):
        rows_of = sub_wide[:, 0 : q.shape[1]]
        return (
            pltpu.roll(jnp.where(rows_of == 0, beyond, q), TILE - 1, 0),
            pltpu.roll(jnp.where(rows_of == TILE - 1, below, q), 1, 0),
        )

    def add_up(ref, base, r):
        total = ref[base, pl.ds(r, TILE), :]
        for k in range(1, LEV):
            total = total + ref[base + k, pl.ds(r, TILE), :]
        return total

    def merid_tile(src, merid, t):
        r = pl.multiple_of(t * TILE, TILE)
        merid[pl.ds(r, TILE), :] = add_up(src, 1 + LEV, r)

    def surface_tile(src, merid, surface, t):
        r, before, after = starts(t)
        e, w = east_west(add_up(src, 1, r), wide)
        n, s = north_south(
            merid[pl.ds(r, TILE), :], merid[pl.ds(before, TILE), :], merid[pl.ds(after, TILE), :]
        )
        divergence = (e - w) + (n - s)
        now = pl.ds(r, TILE)
        surface[now, :] = field[OCEAN, now, :] * (
            src[0, now, :] - (divergence_gain / LEV) * field[DEPTH, now, :] * divergence
        )

    def update_tile(src, surface, t, width, write):
        r, before, after = starts(t)
        now, below, beyond = pl.ds(r, TILE), pl.ds(before, TILE), pl.ds(after, TILE)

        def around(ref, *index):
            whole_q = ref[(*index, now, slice(None))]
            q = whole_q[:, 0:width]
            e, w = east_west(whole_q, width)
            n, s = north_south(
                q, ref[(*index, below, slice(0, width))], ref[(*index, beyond, slice(0, width))]
            )
            return q, e, w, n, s

        new_surface, e, w, n, s = around(surface)
        slope_east = pressure_gain * (e - w)
        slope_north = pressure_gain * (n - s)
        ocean = field[OCEAN, now, 0:width]
        rotation = field[ROT, now, 0:width]
        write(0, r, new_surface)
        for k in range(LEV):
            mixing = field[DIFF + k, now, 0:width]
            u, ue, uw, un, us = around(src, 1 + k)
            v, ve, vw, vn, vs = around(src, 1 + LEV + k)
            c, ce, cw, cn, cs = around(src, 1 + 2 * LEV + k)
            heat_east = ce - cw
            heat_north = cn - cs
            new_u = ocean * (
                u + rotation * v - slope_east - buoyancy_gain * heat_east
                + mixing * (((ue + uw) + (un + us)) - 4.0 * u)
            )
            new_v = ocean * (
                v - rotation * u - slope_north - buoyancy_gain * heat_north
                + mixing * (((ve + vw) + (vn + vs)) - 4.0 * v)
            )
            new_c = ocean * (
                c + mixing * (((ce + cw) + (cn + cs)) - 4.0 * c)
                - advection_gain * (new_u * heat_east + new_v * heat_north)
            )
            write(1 + k, r, new_u)
            write(1 + LEV + k, r, new_v)
            write(1 + 2 * LEV + k, r, new_c)

    def run_steps(src, east, west, count, dst, arrive, leave):
        def middle_write(channel, r, value):
            middle[channel, pl.ds(r, TILE), :] = value

        def last_write(channel, r, value):
            dst[channel, pl.ds(r - TILE, TILE), :] = value

        def body(i, carry):
            @pl.when(i < tall_tiles)
            def _():
                @pl.when((i >= 1) & (i <= tiles))
                def _():
                    arrive(i - 1)

                edge_columns(src, east, west, count, i)
                merid_tile(src, merid_one, i)

            @pl.when((i >= 1) & (i <= tall_tiles))
            def _():
                surface_tile(src, merid_one, surface_one, i - 1)

            @pl.when((i >= 2) & (i <= tall_tiles + 1))
            def _():
                update_tile(src, surface_one, i - 2, wide, middle_write)
                merid_tile(middle, merid_two, i - 2)

            @pl.when((i >= 3) & (i <= tall_tiles + 2))
            def _():
                surface_tile(middle, merid_two, surface_two, i - 3)

            @pl.when(i >= 5)
            def _():
                update_tile(middle, surface_two, i - 4, columns, last_write)
                leave(i - 5)

            return carry

        lax.fori_loop(0, tall_tiles + 3, body, 0)

    def part(t):
        return pl.ds(pl.multiple_of(t * TILE, TILE), TILE)

    def to_pair(t):
        return pltpu.make_async_remote_copy(
            src_ref=control.at[:, part(t), :], dst_ref=control.at[:, part(t), :],
            send_sem=cast_send.at[t], recv_sem=cast_recv.at[t],
            device_id=to_member(me + 1), device_id_type=MESH,
        )

    def save(t, which):
        src, dst = (own, own_out) if which == 0 else (control, control_out)
        return pltpu.make_async_copy(src.at[:, part(t), :], dst.at[:, part(t), :], out_sem.at[which, t])

    def control_done(t):
        @pl.when(has_pair)
        def _():
            to_pair(t).start()

        save(t, 1).start()

    def compare(t):
        total = None
        for k in range(channels):
            d = own[k, part(t), :] - control[k, part(t), :]
            total = d * d if total is None else total + d * d
        r = pl.multiple_of(t * TILE, TILE)
        add_regions(squares, r, field[OCEAN, pl.ds(r + TILE, TILE), 0:columns] * total)

    def own_leave(t):
        save(t, 0).start()

        @pl.when(me == 0)
        def _():
            for k in range(channels):
                control[k, part(t), :] = own[k, part(t), :]
            control_done(t)

    edge_rows(field, from_north, from_south, fields // 2)
    run_steps(field, from_east, from_west, fields, own, lambda t: None, own_leave)

    @pl.when(even & (me > 0))
    def _():
        raw_rims[0].wait_recv()
        raw_rims[1].wait_recv()

        @pl.when(has_north)
        def _():
            raw_rims[2].wait_recv()

        @pl.when(has_south)
        def _():
            raw_rims[3].wait_recv()

        @pl.when(has_next)
        def _():
            start_rims(raw_rims)

        @pl.when(jnp.logical_not(has_north))
        def _():
            raw_north[...] = jnp.zeros_like(raw_north)

        @pl.when(jnp.logical_not(has_south))
        def _():
            raw_south[...] = jnp.zeros_like(raw_south)

        edge_rows(raw, raw_north, raw_south, pairs)

        def arrive(t):
            hand_down(raw, t).wait_recv()

            @pl.when(has_next)
            def _():
                hand_down(raw, t).start()

        def leave(t):
            control_done(t)
            compare(t)

        run_steps(raw, raw_east, raw_west, channels, control, arrive, leave)

    @pl.when(jnp.logical_not(even))
    def _():
        def body(t, carry):
            to_pair(t).wait_recv()
            save(t, 1).start()
            compare(t)
            return carry

        lax.fori_loop(0, tiles, body, 0)

    share(squares, 1)
    count_sum = collect(0)

    @pl.when(has_next)
    def _():
        for copy in raw_rims[0:2]:
            copy.wait_send()

        @pl.when(has_north)
        def _():
            raw_rims[2].wait_send()

        @pl.when(has_south)
        def _():
            raw_rims[3].wait_send()

    def finish(t, carry):
        save(t, 0).wait()
        save(t, 1).wait()

        @pl.when(has_next)
        def _():
            hand_down(raw, t).wait_send()

        @pl.when(has_pair)
        def _():
            to_pair(t).wait_send()

        return carry

    lax.fori_loop(0, tiles, finish, 0)
    square_sum = collect(1)
    growth = jnp.sqrt(square_sum / (count_sum * channels) + epsilon)
    growth_out[...] = jnp.broadcast_to(growth, growth_out.shape)


def breed_kernel(target, region, own, control, growth_in, bred, growth):
    regions = growth_in.shape[0]
    channels, rows, columns = own.shape
    ids = region[...]
    factor = jnp.zeros(ids.shape, jnp.float32)
    for k in range(regions):
        value = target[k] / growth_in[k : k + 1, :]
        value = jnp.concatenate([value] * (columns // LANES), axis=1)
        factor = jnp.where(ids == k, jnp.broadcast_to(value, ids.shape), factor)
    for k in range(channels):
        base = control[k]
        bred[k] = base + factor * (own[k] - base)
    shape = growth_in.shape
    diagonal = lax.broadcasted_iota(jnp.int32, shape, 0) == lax.broadcasted_iota(jnp.int32, shape, 1)
    line = jnp.sum(jnp.where(diagonal, growth_in[...], 0.0), axis=0, keepdims=True)
    growth[...] = line[:, 0 : growth.shape[1]]


def per_device(
    sizes, member_state, column_depth, rotation, diffusivity, ocean_mask, region_id, target_rms
):
    members, lons, lats = sizes
    _, channels, rows, columns = member_state.shape
    regions = target_rms.shape[0]
    fields = channels + 3 + LEV
    tall, wide = rows + 2 * TILE, columns + LANES
    tiles = rows // TILE
    group = lons * lats
    f32 = jnp.float32
    anywhere = pl.BlockSpec(memory_space=pl.ANY)
    own, control, growth_wide = pl.pallas_call(
        functools.partial(cycle_kernel, sizes),
        out_shape=(
            jax.ShapeDtypeStruct((channels, rows, columns), f32),
            jax.ShapeDtypeStruct((channels, rows, columns), f32),
            jax.ShapeDtypeStruct((regions, LANES), f32),
        ),
        in_specs=[anywhere] * 6,
        out_specs=(anywhere, anywhere, pl.BlockSpec(memory_space=pltpu.VMEM)),
        scratch_shapes=[
            pltpu.VMEM((fields, tall, wide), f32),
            pltpu.VMEM((channels, tall, wide), f32),
            pltpu.VMEM((channels, tall, wide), f32),
            pltpu.VMEM((channels, rows, columns), f32),
            pltpu.VMEM((channels, rows, columns), f32),
            pltpu.VMEM((rows, columns), jnp.int32),
            pltpu.VMEM((rows, columns), jnp.int32),
            pltpu.VMEM((tall, wide), f32),
            pltpu.VMEM((tall, wide), f32),
            pltpu.VMEM((tall, wide), f32),
            pltpu.VMEM((tall, wide), f32),
            pltpu.VMEM((rows, LANES), f32),
            pltpu.VMEM((rows, LANES), f32),
            pltpu.VMEM((tall, LANES), f32),
            pltpu.VMEM((tall, LANES), f32),
            pltpu.VMEM((fields // 2, TILE, columns), f32),
            pltpu.VMEM((fields // 2, TILE, columns), f32),
            pltpu.VMEM((fields // 2, TILE, columns), f32),
            pltpu.VMEM((fields // 2, TILE, columns), f32),
            pltpu.VMEM((tall, LANES), f32),
            pltpu.VMEM((tall, LANES), f32),
            pltpu.VMEM((channels // 2, TILE, columns), f32),
            pltpu.VMEM((channels // 2, TILE, columns), f32),
            pltpu.VMEM((regions, TILE, LANES), f32),
            pltpu.VMEM((regions, TILE, LANES), f32),
            pltpu.VMEM((2, group, regions, LANES), f32),
            pltpu.SemaphoreType.DMA((6,)),
            pltpu.SemaphoreType.DMA((8,)),
            pltpu.SemaphoreType.DMA((8,)),
            pltpu.SemaphoreType.DMA((tiles,)),
            pltpu.SemaphoreType.DMA((tiles,)),
            pltpu.SemaphoreType.DMA((4,)),
            pltpu.SemaphoreType.DMA((4,)),
            pltpu.SemaphoreType.DMA((tiles,)),
            pltpu.SemaphoreType.DMA((tiles,)),
            pltpu.SemaphoreType.DMA((2, tiles)),
            pltpu.SemaphoreType.DMA((2, group - 1)),
            pltpu.SemaphoreType.DMA((2, group - 1)),
        ],
        compiler_params=pltpu.CompilerParams(collective_id=0, has_side_effects=True),
    )(
        member_state.reshape(channels, rows, columns),
        column_depth, rotation, diffusivity, ocean_mask, region_id,
    )
    block = 32 if rows % 32 == 0 else rows
    volume = pl.BlockSpec((channels, block, columns), lambda i: (0, i, 0))
    bred, growth = pl.pallas_call(
        breed_kernel,
        grid=(rows // block,),
        out_shape=(
            jax.ShapeDtypeStruct((channels, rows, columns), f32),
            jax.ShapeDtypeStruct((1, regions), f32),
        ),
        in_specs=[
            pl.BlockSpec(memory_space=pltpu.SMEM),
            pl.BlockSpec((block, columns), lambda i: (i, 0)),
            volume,
            volume,
            pl.BlockSpec((regions, LANES), lambda i: (0, 0)),
        ],
        out_specs=(volume, pl.BlockSpec((1, regions), lambda i: (0, 0))),
    )(target_rms, region_id, own, control, growth_wide)
    return (bred[None], growth)


def solution(mesh):
    sizes = (mesh.shape["member"], mesh.shape["lon"], mesh.shape["lat"])
    return jax.shard_map(
        functools.partial(per_device, sizes),
        mesh=mesh,
        in_specs=(
            P("member", None, "lat", "lon"),
            P("lat", "lon"),
            P("lat", "lon"),
            P(None, "lat", "lon"),
            P("lat", "lon"),
            P("lat", "lon"),
            P(),
        ),
        out_specs=(P("member", None, "lat", "lon"), P("member", None)),
        check_vma=False,
    )
```

```python
import functools

import jax
import jax.numpy as jnp
from jax import lax
from jax.experimental import pallas as pl
from jax.experimental.pallas import tpu as pltpu
from jax.sharding import PartitionSpec as P

LEV = 5
STEPS = 2
MARGIN = 2 * STEPS
TILE = 8
LANES = 128
EARLY = 9
KERNEL_BYTES = 56 * 2**20
BREED_BYTES = 16 * 2**20

divergence_gain = 0.25
pressure_gain = 0.25
buoyancy_gain = 0.1
advection_gain = 0.05
epsilon = 1e-06

MESH = pl.DeviceIdType.MESH


def cycle_kernel(
    sizes,
    state_in, depth_in, rotation_in, diffusivity_in, mask_in, region_in,
    own, control, growth_out,
    field, middle, raw, mask, region,
    surface_one, surface_two, merid_one, merid_two,
    send_east, send_west, from_east, from_west,
    send_north, send_south, from_north, from_south,
    raw_east, raw_west, raw_north, raw_south,
    squares, counts, gathered,
    in_sem, halo_send, halo_recv, raw_send, raw_recv, rim_send, rim_recv,
    cast_send, cast_recv, sum_send, sum_recv,
):
    members, lons, lats = sizes
    channels, rows, columns = state_in.shape
    regions = growth_out.shape[0]
    fields = field.shape[0]
    wide = columns + LANES
    tiles = rows // TILE
    tall_tiles = tiles + 2
    DEPTH, ROT, OCEAN, DIFF = channels, channels + 1, channels + 2, channels + 3

    me = lax.axis_index("member")
    lon = lax.axis_index("lon")
    lat = lax.axis_index("lat")

    def at(dlat, dlon):
        return {
            "member": me,
            "lon": lax.rem(lon + dlon + lons, lons),
            "lat": lax.rem(lat + dlat + lats, lats),
        }

    def to_member(other):
        return {"member": other, "lon": lon, "lat": lat}

    inner = (slice(TILE, TILE + rows), slice(0, columns))
    loads = [
        pltpu.make_async_copy(state_in, field.at[(slice(0, channels),) + inner], in_sem.at[0]),
        pltpu.make_async_copy(depth_in, field.at[(DEPTH,) + inner], in_sem.at[1]),
        pltpu.make_async_copy(rotation_in, field.at[(ROT,) + inner], in_sem.at[2]),
        pltpu.make_async_copy(diffusivity_in, field.at[(slice(DIFF, fields),) + inner], in_sem.at[3]),
        pltpu.make_async_copy(mask_in, mask, in_sem.at[4]),
        pltpu.make_async_copy(region_in, region, in_sem.at[5]),
    ]
    for load in loads:
        load.start()

    peers = [(a, b) for a in range(lats) for b in range(lons) if (a, b) != (0, 0)]
    barrier = pltpu.get_barrier_semaphore()
    for a, b in peers:
        pl.semaphore_signal(barrier, inc=1, device_id=at(a, b), device_id_type=MESH)
    even = lax.rem(me, 2) == 0
    has_pair = even & (me + 1 < members)
    has_next = even & (me + 2 < members)
    parent = jnp.where(even, me - 2, me - 1)

    @pl.when(me > 0)
    def _():
        pl.semaphore_signal(barrier, inc=1, device_id=to_member(parent), device_id_type=MESH)

    pl.semaphore_wait(
        barrier, len(peers) + has_pair.astype(jnp.int32) + has_next.astype(jnp.int32)
    )

    for load in loads:
        load.wait()

    early = min(EARLY, tiles)

    def cells(ref, t):
        return ref.at[0:channels, pl.ds(pl.multiple_of((t + 1) * TILE, TILE), TILE), 0:columns]

    def hand_down(src, t):
        return pltpu.make_async_remote_copy(
            src_ref=cells(src, t), dst_ref=cells(raw, t),
            send_sem=raw_send.at[t], recv_sem=raw_recv.at[t],
            device_id=to_member(me + 2), device_id_type=MESH,
        )

    def hand_down_some(begin, end):
        @pl.when((me == 0) & has_next)
        def _():
            def body(t, carry):
                hand_down(field, t).start()
                return carry

            lax.fori_loop(begin, end, body, 0)

    hand_down_some(0, early)

    lane = lax.broadcasted_iota(jnp.int32, (TILE, LANES), 1)
    sub = lax.broadcasted_iota(jnp.int32, (TILE, columns), 0)
    zero_tile = jnp.zeros((TILE, LANES), jnp.float32)

    def make_ocean(t, carry):
        r = pl.multiple_of(t * TILE, TILE)
        field[OCEAN, pl.ds(r + TILE, TILE), 0:columns] = mask[pl.ds(r, TILE), :].astype(jnp.float32)
        return carry

    lax.fori_loop(0, tiles, make_ocean, 0)

    for k in range(fields // 2):
        a, b = 2 * k, 2 * k + 1
        top = slice(rows, rows + TILE)
        low = slice(TILE, 2 * TILE)
        half = TILE // 2
        send_north[k] = jnp.where(
            sub < half, pltpu.roll(field[a, top, 0:columns], half, 0), field[b, top, 0:columns]
        )
        send_south[k] = jnp.where(
            sub < half, field[a, low, 0:columns], pltpu.roll(field[b, low, 0:columns], half, 0)
        )

    def remote(src, dst, index, device):
        return pltpu.make_async_remote_copy(
            src_ref=src, dst_ref=dst, send_sem=halo_send.at[index], recv_sem=halo_recv.at[index],
            device_id=device, device_id_type=MESH,
        )

    has_north = lat < lats - 1
    has_south = lat > 0
    whole = slice(TILE, TILE + rows)
    last = slice(rows - TILE, rows)
    first = slice(0, TILE)
    above = slice(rows + TILE, rows + 2 * TILE)
    north = [remote(send_north, from_south, 0, at(1, 0))]
    south = [remote(send_south, from_north, 1, at(-1, 0))]
    sideways = [
        remote(send_east, from_west.at[whole], 2, at(0, 1)),
        remote(send_west, from_east.at[whole], 3, at(0, -1)),
    ]
    north_corners = [
        remote(send_east.at[last], from_west.at[first], 4, at(1, 1)),
        remote(send_west.at[last], from_east.at[first], 5, at(1, -1)),
    ]
    south_corners = [
        remote(send_east.at[first], from_west.at[above], 6, at(-1, 1)),
        remote(send_west.at[first], from_east.at[above], 7, at(-1, -1)),
    ]

    @pl.when(has_north)
    def _():
        for copy in north:
            copy.start()

    @pl.when(has_south)
    def _():
        for copy in south:
            copy.start()

    def pack(t, carry):
        r = pl.multiple_of(t * TILE, TILE)
        east, west = zero_tile, zero_tile
        for f in range(fields):
            here = (lane >= MARGIN * f) & (lane < MARGIN * (f + 1))
            edge = field[f, pl.ds(r + TILE, TILE), columns - LANES : columns]
            east = jnp.where(here, pltpu.roll(edge, (MARGIN * f + MARGIN) % LANES, 1), east)
            edge = field[f, pl.ds(r + TILE, TILE), 0:LANES]
            west = jnp.where(here, pltpu.roll(edge, MARGIN * f, 1) if f else edge, west)
        send_east[pl.ds(r, TILE), :] = east
        send_west[pl.ds(r, TILE), :] = west
        return carry

    lax.fori_loop(0, tiles, pack, 0)
    for copy in sideways:
        copy.start()

    @pl.when(has_north)
    def _():
        for copy in north_corners:
            copy.start()

    @pl.when(has_south)
    def _():
        for copy in south_corners:
            copy.start()

    def clear(ref):
        for k in range(regions):
            ref[k] = zero_tile

    def add_regions(ref, r, value):
        ids = region[pl.ds(r, TILE), :]
        for k in range(regions):
            picked = jnp.where(ids == k, value, 0.0)
            total = picked[:, 0:LANES]
            for c in range(LANES, columns, LANES):
                total = total + picked[:, c : c + LANES]
            ref[k] = ref[k] + total

    def share(ref, which):
        gathered[which, 0] = jnp.sum(ref[...], axis=1)
        for p, (a, b) in enumerate(peers):
            pltpu.make_async_remote_copy(
                src_ref=gathered.at[which, 0], dst_ref=gathered.at[which, p + 1],
                send_sem=sum_send.at[which, p], recv_sem=sum_recv.at[which, p],
                device_id=at(a, b), device_id_type=MESH,
            ).start()

    def collect(which):
        for p, (a, b) in enumerate(peers):
            pltpu.make_async_remote_copy(
                src_ref=gathered.at[which, 0], dst_ref=gathered.at[which, p + 1],
                send_sem=sum_send.at[which, p], recv_sem=sum_recv.at[which, p],
                device_id=at(a, b), device_id_type=MESH,
            ).wait()
        total = gathered[which, 0]
        for p in range(len(peers)):
            total = total + gathered[which, p + 1]
        return jnp.sum(total, axis=1, keepdims=True)

    clear(squares)
    clear(counts)

    def count(t, carry):
        r = pl.multiple_of(t * TILE, TILE)
        add_regions(counts, r, field[OCEAN, pl.ds(r + TILE, TILE), 0:columns])
        return carry

    lax.fori_loop(0, tiles, count, 0)
    share(counts, 0)

    for copy in sideways:
        copy.wait()

    @pl.when(has_north)
    def _():
        for copy in north + north_corners:
            copy.wait_send()
        for copy in south + south_corners:
            copy.wait_recv()

    @pl.when(has_south)
    def _():
        for copy in south + south_corners:
            copy.wait_send()
        for copy in north + north_corners:
            copy.wait_recv()

    @pl.when(jnp.logical_not(has_north))
    def _():
        from_north[...] = jnp.zeros_like(from_north)
        from_east[above, :] = zero_tile
        from_west[above, :] = zero_tile

    @pl.when(jnp.logical_not(has_south))
    def _():
        from_south[...] = jnp.zeros_like(from_south)
        from_east[first, :] = zero_tile
        from_west[first, :] = zero_tile

    pairs = channels // 2

    def rims(east, west, above_rows, below_rows):
        def rim(src, dst, index):
            return pltpu.make_async_remote_copy(
                src_ref=src, dst_ref=dst, send_sem=rim_send.at[index], recv_sem=rim_recv.at[index],
                device_id=to_member(me + 2), device_id_type=MESH,
            )

        return (
            rim(east, raw_east, 0),
            rim(west, raw_west, 1),
            rim(above_rows, raw_north, 2),
            rim(below_rows, raw_south, 3),
        )

    own_rims = rims(from_east, from_west, from_north.at[0:pairs], from_south.at[0:pairs])
    raw_rims = rims(raw_east, raw_west, raw_north, raw_south)

    def start_rims(copies):
        copies[0].start()
        copies[1].start()

        @pl.when(has_north)
        def _():
            copies[2].start()

        @pl.when(has_south)
        def _():
            copies[3].start()

    @pl.when((me == 0) & has_next)
    def _():
        start_rims(own_rims)

    hand_down_some(early, tiles)

    def edge_rows(ref, above_rows, below_rows, count):
        for k in range(count):
            a, b = 2 * k, 2 * k + 1
            ref[a, first, 0:columns] = pltpu.roll(below_rows[k], TILE // 2, 0)
            ref[b, first, 0:columns] = below_rows[k]
            ref[a, above, 0:columns] = above_rows[k]
            ref[b, above, 0:columns] = pltpu.roll(above_rows[k], TILE // 2, 0)

    def edge_columns(ref, east_ref, west_ref, count, t):
        r = pl.multiple_of(t * TILE, TILE)
        east = east_ref[pl.ds(r, TILE), :]
        west = west_ref[pl.ds(r, TILE), :]
        for f in range(count):
            to_first = pltpu.roll(east, LANES - MARGIN * f, 1) if f else east
            to_last = pltpu.roll(west, LANES - MARGIN - MARGIN * f, 1)
            ref[f, pl.ds(r, TILE), columns:wide] = jnp.where(lane < MARGIN, to_first, to_last)

    sub_wide = lax.broadcasted_iota(jnp.int32, (TILE, wide), 0)

    def starts(t):
        r = pl.multiple_of(t * TILE, TILE)
        before = pl.multiple_of(jnp.maximum(t - 1, 0) * TILE, TILE)
        after = pl.multiple_of(jnp.minimum(t + 1, tiles + 1) * TILE, TILE)
        return r, before, after

    def east_west(q, width):
        return (
            pltpu.roll(q, wide - 1, 1)[:, 0:width],
            pltpu.roll(q, 1, 1)[:, 0:width],
        )

    def north_south(q, below, beyond):
        rows_of = sub_wide[:, 0 : q.shape[1]]
        return (
            pltpu.roll(jnp.where(rows_of == 0, beyond, q), TILE - 1, 0),
            pltpu.roll(jnp.where(rows_of == TILE - 1, below, q), 1, 0),
        )

    def add_up(ref, base, r):
        total = ref[base, pl.ds(r, TILE), :]
        for k in range(1, LEV):
            total = total + ref[base + k, pl.ds(r, TILE), :]
        return total

    def merid_tile(src, merid, t):
        r = pl.multiple_of(t * TILE, TILE)
        merid[pl.ds(r, TILE), :] = add_up(src, 1 + LEV, r)

    def surface_tile(src, merid, surface, t):
        r, before, after = starts(t)
        e, w = east_west(add_up(src, 1, r), wide)
        n, s = north_south(
            merid[pl.ds(r, TILE), :], merid[pl.ds(before, TILE), :], merid[pl.ds(after, TILE), :]
        )
        divergence = (e - w) + (n - s)
        now = pl.ds(r, TILE)
        surface[now, :] = field[OCEAN, now, :] * (
            src[0, now, :] - (divergence_gain / LEV) * field[DEPTH, now, :] * divergence
        )

    def update_tile(src, surface, t, width, write):
        r, before, after = starts(t)
        now, below, beyond = pl.ds(r, TILE), pl.ds(before, TILE), pl.ds(after, TILE)

        def around(ref, *index):
            whole_q = ref[(*index, now, slice(None))]
            q = whole_q[:, 0:width]
            e, w = east_west(whole_q, width)
            n, s = north_south(
                q, ref[(*index, below, slice(0, width))], ref[(*index, beyond, slice(0, width))]
            )
            return q, e, w, n, s

        new_surface, e, w, n, s = around(surface)
        slope_east = pressure_gain * (e - w)
        slope_north = pressure_gain * (n - s)
        ocean = field[OCEAN, now, 0:width]
        rotation = field[ROT, now, 0:width]
        write(0, r, new_surface)
        for k in range(LEV):
            mixing = field[DIFF + k, now, 0:width]
            u, ue, uw, un, us = around(src, 1 + k)
            v, ve, vw, vn, vs = around(src, 1 + LEV + k)
            c, ce, cw, cn, cs = around(src, 1 + 2 * LEV + k)
            heat_east = ce - cw
            heat_north = cn - cs
            new_u = ocean * (
                u + rotation * v - slope_east - buoyancy_gain * heat_east
                + mixing * (((ue + uw) + (un + us)) - 4.0 * u)
            )
            new_v = ocean * (
                v - rotation * u - slope_north - buoyancy_gain * heat_north
                + mixing * (((ve + vw) + (vn + vs)) - 4.0 * v)
            )
            new_c = ocean * (
                c + mixing * (((ce + cw) + (cn + cs)) - 4.0 * c)
                - advection_gain * (new_u * heat_east + new_v * heat_north)
            )
            write(1 + k, r, new_u)
            write(1 + LEV + k, r, new_v)
            write(1 + 2 * LEV + k, r, new_c)

    def run_steps(src, east, west, count, dst, arrive, leave):
        def middle_write(channel, r, value):
            middle[channel, pl.ds(r, TILE), :] = value

        def last_write(channel, r, value):
            dst[channel, pl.ds(r - TILE, TILE), :] = value

        def body(i, carry):
            @pl.when(i < tall_tiles)
            def _():
                @pl.when((i >= 1) & (i <= tiles))
                def _():
                    arrive(i - 1)

                edge_columns(src, east, west, count, i)
                merid_tile(src, merid_one, i)

            @pl.when((i >= 1) & (i <= tall_tiles))
            def _():
                surface_tile(src, merid_one, surface_one, i - 1)

            @pl.when((i >= 2) & (i <= tall_tiles + 1))
            def _():
                update_tile(src, surface_one, i - 2, wide, middle_write)
                merid_tile(middle, merid_two, i - 2)

            @pl.when((i >= 3) & (i <= tall_tiles + 2))
            def _():
                surface_tile(middle, merid_two, surface_two, i - 3)

            @pl.when(i >= 5)
            def _():
                update_tile(middle, surface_two, i - 4, columns, last_write)
                leave(i - 5)

            return carry

        lax.fori_loop(0, tall_tiles + 3, body, 0)

    def part(t):
        return pl.ds(pl.multiple_of(t * TILE, TILE), TILE)

    def to_pair(t):
        return pltpu.make_async_remote_copy(
            src_ref=control.at[:, part(t), :], dst_ref=control.at[:, part(t), :],
            send_sem=cast_send.at[t], recv_sem=cast_recv.at[t],
            device_id=to_member(me + 1), device_id_type=MESH,
        )

    def control_done(t):
        @pl.when(has_pair)
        def _():
            to_pair(t).start()

    def compare(t):
        total = None
        for k in range(channels):
            d = own[k, part(t), :] - control[k, part(t), :]
            total = d * d if total is None else total + d * d
        r = pl.multiple_of(t * TILE, TILE)
        add_regions(squares, r, field[OCEAN, pl.ds(r + TILE, TILE), 0:columns] * total)

    def own_leave(t):
        @pl.when(me == 0)
        def _():
            for k in range(channels):
                control[k, part(t), :] = own[k, part(t), :]
            control_done(t)

    edge_rows(field, from_north, from_south, fields // 2)
    run_steps(field, from_east, from_west, fields, own, lambda t: None, own_leave)

    @pl.when(even & (me > 0))
    def _():
        raw_rims[0].wait_recv()
        raw_rims[1].wait_recv()

        @pl.when(has_north)
        def _():
            raw_rims[2].wait_recv()

        @pl.when(has_south)
        def _():
            raw_rims[3].wait_recv()

        @pl.when(has_next)
        def _():
            start_rims(raw_rims)

        @pl.when(jnp.logical_not(has_north))
        def _():
            raw_north[...] = jnp.zeros_like(raw_north)

        @pl.when(jnp.logical_not(has_south))
        def _():
            raw_south[...] = jnp.zeros_like(raw_south)

        edge_rows(raw, raw_north, raw_south, pairs)

        def arrive(t):
            hand_down(raw, t).wait_recv()

            @pl.when(has_next)
            def _():
                hand_down(raw, t).start()

        def leave(t):
            control_done(t)
            compare(t)

        run_steps(raw, raw_east, raw_west, channels, control, arrive, leave)

    @pl.when(jnp.logical_not(even))
    def _():
        def body(t, carry):
            to_pair(t).wait_recv()
            compare(t)
            return carry

        lax.fori_loop(0, tiles, body, 0)

    share(squares, 1)
    count_sum = collect(0)

    @pl.when(has_next)
    def _():
        for copy in raw_rims[0:2]:
            copy.wait_send()

        @pl.when(has_north)
        def _():
            raw_rims[2].wait_send()

        @pl.when(has_south)
        def _():
            raw_rims[3].wait_send()

    def finish(t, carry):
        @pl.when(has_next)
        def _():
            hand_down(raw, t).wait_send()

        @pl.when(has_pair)
        def _():
            to_pair(t).wait_send()

        return carry

    lax.fori_loop(0, tiles, finish, 0)
    square_sum = collect(1)
    growth = jnp.sqrt(square_sum / (count_sum * channels) + epsilon)
    growth_out[...] = jnp.broadcast_to(growth, growth_out.shape)


def breed_kernel(target, region, own, control, growth_in, bred, growth):
    regions = growth_in.shape[0]
    channels, block, columns = bred.shape
    now = pl.ds(pl.multiple_of(pl.program_id(0) * block, TILE), block)
    ids = region[...]
    factor = jnp.zeros(ids.shape, jnp.float32)
    for k in range(regions):
        value = target[k] / growth_in[k : k + 1, :]
        value = jnp.concatenate([value] * (columns // LANES), axis=1)
        factor = jnp.where(ids == k, jnp.broadcast_to(value, ids.shape), factor)
    for k in range(channels):
        base = control[k, now, :]
        bred[k] = base + factor * (own[k, now, :] - base)
    shape = growth_in.shape
    diagonal = lax.broadcasted_iota(jnp.int32, shape, 0) == lax.broadcasted_iota(jnp.int32, shape, 1)
    line = jnp.sum(jnp.where(diagonal, growth_in[...], 0.0), axis=0, keepdims=True)
    growth[...] = line[:, 0 : growth.shape[1]]


def per_device(
    sizes, member_state, column_depth, rotation, diffusivity, ocean_mask, region_id, target_rms
):
    members, lons, lats = sizes
    _, channels, rows, columns = member_state.shape
    regions = target_rms.shape[0]
    fields = channels + 3 + LEV
    tall, wide = rows + 2 * TILE, columns + LANES
    tiles = rows // TILE
    group = lons * lats
    f32 = jnp.float32
    anywhere = pl.BlockSpec(memory_space=pl.ANY)
    resident = pl.BlockSpec(memory_space=pltpu.VMEM)
    own, control, growth_wide = pl.pallas_call(
        functools.partial(cycle_kernel, sizes),
        out_shape=(
            pltpu.VMEM((channels, rows, columns), f32),
            pltpu.VMEM((channels, rows, columns), f32),
            pltpu.VMEM((regions, LANES), f32),
        ),
        in_specs=[anywhere] * 6,
        out_specs=(resident,) * 3,
        scratch_shapes=[
            pltpu.VMEM((fields, tall, wide), f32),
            pltpu.VMEM((channels, tall, wide), f32),
            pltpu.VMEM((channels, tall, wide), f32),
            pltpu.VMEM((rows, columns), jnp.int32),
            pltpu.VMEM((rows, columns), jnp.int32),
            pltpu.VMEM((tall, wide), f32),
            pltpu.VMEM((tall, wide), f32),
            pltpu.VMEM((tall, wide), f32),
            pltpu.VMEM((tall, wide), f32),
            pltpu.VMEM((rows, LANES), f32),
            pltpu.VMEM((rows, LANES), f32),
            pltpu.VMEM((tall, LANES), f32),
            pltpu.VMEM((tall, LANES), f32),
            pltpu.VMEM((fields // 2, TILE, columns), f32),
            pltpu.VMEM((fields // 2, TILE, columns), f32),
            pltpu.VMEM((fields // 2, TILE, columns), f32),
            pltpu.VMEM((fields // 2, TILE, columns), f32),
            pltpu.VMEM((tall, LANES), f32),
            pltpu.VMEM((tall, LANES), f32),
            pltpu.VMEM((channels // 2, TILE, columns), f32),
            pltpu.VMEM((channels // 2, TILE, columns), f32),
            pltpu.VMEM((regions, TILE, LANES), f32),
            pltpu.VMEM((regions, TILE, LANES), f32),
            pltpu.VMEM((2, group, regions, LANES), f32),
            pltpu.SemaphoreType.DMA((6,)),
            pltpu.SemaphoreType.DMA((8,)),
            pltpu.SemaphoreType.DMA((8,)),
            pltpu.SemaphoreType.DMA((tiles,)),
            pltpu.SemaphoreType.DMA((tiles,)),
            pltpu.SemaphoreType.DMA((4,)),
            pltpu.SemaphoreType.DMA((4,)),
            pltpu.SemaphoreType.DMA((tiles,)),
            pltpu.SemaphoreType.DMA((tiles,)),
            pltpu.SemaphoreType.DMA((2, group - 1)),
            pltpu.SemaphoreType.DMA((2, group - 1)),
        ],
        compiler_params=pltpu.CompilerParams(
            collective_id=0, has_side_effects=True, vmem_limit_bytes=KERNEL_BYTES
        ),
    )(
        member_state.reshape(channels, rows, columns),
        column_depth, rotation, diffusivity, ocean_mask, region_id,
    )
    block = 2 * TILE if rows % (2 * TILE) == 0 else TILE
    bred, growth = pl.pallas_call(
        breed_kernel,
        grid=(rows // block,),
        out_shape=(
            jax.ShapeDtypeStruct((channels, rows, columns), f32),
            jax.ShapeDtypeStruct((1, regions), f32),
        ),
        in_specs=[
            pl.BlockSpec(memory_space=pltpu.SMEM),
            pl.BlockSpec((block, columns), lambda i: (i, 0)),
            resident,
            resident,
            resident,
        ],
        out_specs=(
            pl.BlockSpec((channels, block, columns), lambda i: (0, i, 0)),
            pl.BlockSpec((1, regions), lambda i: (0, 0)),
        ),
        compiler_params=pltpu.CompilerParams(vmem_limit_bytes=BREED_BYTES),
    )(target_rms, region_id, own, control, growth_wide)
    return (bred[None], growth)


def solution(mesh):
    sizes = (mesh.shape["member"], mesh.shape["lon"], mesh.shape["lat"])
    return jax.shard_map(
        functools.partial(per_device, sizes),
        mesh=mesh,
        in_specs=(
            P("member", None, "lat", "lon"),
            P("lat", "lon"),
            P("lat", "lon"),
            P(None, "lat", "lon"),
            P("lat", "lon"),
            P("lat", "lon"),
            P(),
        ),
        out_specs=(P("member", None, "lat", "lon"), P("member", None)),
        check_vma=False,
    )
```
